256 devices in a mesh: seq: 128 (over x, z, y), head: 2 (over core).
Axes of the slice: x: 4, y: 4, z: 8, core: 2. Of those that a mesh axis runs over, the one named last changes fastest.
Arguments:
- queries: bfloat16 [16384, 512], P('seq', 'head')
- keys_values: bfloat16 [16384, 256], P(('seq', 'head'))
- selected: int32 [128, 3], replicated, may hold values from -1 to 31, as said below
Outputs:
- attended: bfloat16 [16384, 512], P('seq', 'head')
The draws below stay inside these ranges and needn't reach their ends.
Inputs may be any that keep to these rules, and one draw needn't show every extreme that they name: selected[c, 0] = c // 4, the span's own block; selected[c, 1] and selected[c, 2] are two different blocks before it, chosen at random; where fewer than two earlier blocks exist, the missing entries are -1 (column 1 first filled).
All inputs are finite; a program needn't handle non-finite values.
Results may differ from the reference program's by a relative error of at most 0.0052.
Values may be sent and summed in bfloat16 or wider, within the bound.
A program may use at most 64 MiB of HBM per device.

```python
import jax
import jax.numpy as jnp
from jax import lax

DH = 128
HQ = 4
TOK_DEV = 128
GROUP = 4
TOPK = 3
BLOCK = 512
TOKENS = 16384
N_SEQ = 128


def shared_keys(key):
    return jax.random.normal(jax.random.fold_in(key, 11), (TOKENS, 2 * DH), jnp.float32)


def draw_keys_values(key, part):
    return shared_keys(key).astype(jnp.bfloat16)


def draw_queries(key, part):
    normal_rows = jax.random.normal(jax.random.fold_in(key, 23), (TOKENS, HQ * DH), jnp.float32)
    return normal_rows.astype(jnp.bfloat16)


def draw_selected(key, part):
    spans = jnp.arange(N_SEQ, dtype=jnp.int32)
    own_block = spans // GROUP
    first_bits = jax.random.randint(jax.random.fold_in(key, 31), (N_SEQ,), 0, 1 << 20, dtype=jnp.int32)
    second_bits = jax.random.randint(jax.random.fold_in(key, 37), (N_SEQ,), 0, 1 << 20, dtype=jnp.int32)
    first = first_bits % jnp.maximum(own_block, 1)
    second = second_bits % jnp.maximum(own_block - 1, 1)
    second = second + (second >= first).astype(jnp.int32)
    column_one = jnp.where(own_block >= 1, first, -1)
    column_two = jnp.where(own_block >= 2, second, -1)
    return jnp.stack([own_block, column_one, column_two], axis=1).astype(jnp.int32)


def setup_inputs(seed: int = 0) -> dict:
    splits = jax.random.split(jax.random.key(seed), 4)
    queries = draw_queries(jax.random.fold_in(splits[3], 71), 0)
    keys_values = draw_keys_values(jax.random.fold_in(splits[3], 71), 0)
    selected = draw_selected(jax.random.fold_in(splits[3], 71), 0)
    return {"queries": queries, "keys_values": keys_values, "selected": selected}


def part_attend(query_rows, block_kv, query_pos, key_pos):
    keys = block_kv[:, :DH]
    values = block_kv[:, DH:]
    scores = jnp.einsum("nhd,kd->hnk", query_rows, keys) * (DH ** -0.5)
    allowed = key_pos[None, :] <= query_pos[:, None]
    scores = jnp.where(allowed[None], scores, -1e30)
    top = jnp.max(scores, axis=-1)
    expo = jnp.exp(scores - top[..., None])
    total = jnp.sum(expo, axis=-1)
    weights = expo.astype(jnp.bfloat16).astype(jnp.float32)
    outputs = jnp.einsum("hnk,kd->nhd", weights, values) / jnp.transpose(total)[..., None]
    lse = jnp.transpose(top + jnp.log(total))
    return outputs, lse


def reference(queries, keys_values, selected):
    kv_all = keys_values.astype(jnp.float32)

    def one_span(span):
        start = (span * TOK_DEV).astype(jnp.int32)
        rows = lax.dynamic_slice_in_dim(queries, start, TOK_DEV, 0).astype(jnp.float32)
        rows = rows.reshape(TOK_DEV, HQ, DH)
        query_pos = start + jnp.arange(TOK_DEV, dtype=jnp.int32)
        outs_list = []
        lse_list = []
        for column in range(TOPK):
            block_id = selected[span, column]
            safe = jnp.maximum(block_id, 0).astype(jnp.int32)
            kv_start = (safe * BLOCK).astype(jnp.int32)
            block_kv = lax.dynamic_slice_in_dim(kv_all, kv_start, BLOCK, 0)
            key_pos = kv_start + jnp.arange(BLOCK, dtype=jnp.int32)
            outputs, lse = part_attend(rows, block_kv, query_pos, key_pos)
            if column >= 1:
                outputs = lax.optimization_barrier(outputs.astype(jnp.bfloat16)).astype(jnp.float32)
            lse = jnp.where(block_id >= 0, lse, -1e30)
            outs_list.append(outputs)
            lse_list.append(lse)
        lse_all = jnp.stack(lse_list)
        outs_all = jnp.stack(outs_list)
        largest = jnp.max(lse_all, axis=0)
        scale = jnp.exp(lse_all - largest[None])
        merged = jnp.sum(scale[..., None] * outs_all, axis=0) / jnp.sum(scale, axis=0)[..., None]
        return merged.reshape(TOK_DEV, HQ * DH).astype(jnp.bfloat16)

    result = lax.map(one_span, jnp.arange(N_SEQ, dtype=jnp.int32))
    return result.reshape(TOKENS, HQ * DH)
```

```python
import jax
import jax.numpy as jnp
from jax import lax
from jax.experimental import pallas as pl
from jax.experimental.pallas import tpu as pltpu
from jax.sharding import PartitionSpec as P

DH = 128
NX, NZ, NY = 4, 8, 4
ROWS = 64
HALF = ROWS // 2
MESH = pl.DeviceIdType.MESH
NEG = -1e30


def a_next(dx, dz):
    out = []
    if dz == 0:
        if dx == 0:
            out += [("x", 1, 1, 0), ("x", -1, 3, 0), ("x", 2, 2, 0)]
        out += [("z", 1, dx, 1), ("z", -1, dx, 7)]
    elif dz < 3 or (dz == 3 and dx % 2 == 0):
        out += [("z", 1, dx, dz + 1)]
    elif dz > 5 or (dz == 5 and dx % 2 == 1):
        out += [("z", -1, dx, dz - 1)]
    return out


def b_next(dx, dz):
    out = []
    if dx == 0:
        if dz == 0:
            out += [("z", 1, 0, 1), ("z", -1, 0, 7)]
        elif dz < 4:
            out += [("z", 1, 0, dz + 1)]
        elif dz > 5:
            out += [("z", -1, 0, dz - 1)]
        out += [("x", 1, 1, dz), ("x", -1, 3, dz)]
    elif dx == 1 and dz % 2 == 0:
        out += [("x", 1, 2, dz)]
    elif dx == 3 and dz % 2 == 1:
        out += [("x", -1, 2, dz)]
    return out


def levels(follow):
    cost = {(0, 0): 0}
    order = [(0, 0)]
    for node in order:
        for _, step, dx, dz in follow(*node):
            cost[(dx, dz)] = cost[node] + abs(step)
            order.append((dx, dz))
    return cost


def kernel(q_ref, kv_ref, sel_ref, o_ref, kvb, kvown, kvsel, stg, a_send, a_recv, b_send, b_recv, own_send, own_recv,
           y_send, y_recv, p_send, p_recv):
    s = lax.axis_index("seq")
    h = lax.axis_index("head")
    x = s // (NZ * NY)
    z = (s // NY) % NZ
    y = s % NY
    base = s - y

    def dev(axis, step):
        if axis == "x":
            return (((x + step + NX) % NX) * (NZ * NY) + z * NY + y, h)
        if axis == "z":
            return (x * (NZ * NY) + ((z + step + NZ) % NZ) * NY + y, h)
        return (base + (y + step) % NY, h)

    partner = (s, 1 - h)
    near = [dev("x", 1), dev("x", 2), dev("x", 3), dev("z", 1), dev("z", -1), partner]
    for k in range(1, NY):
        near += [dev("y", k), (dev("y", k)[0], 1 - h)]
    barrier = pltpu.get_barrier_semaphore()
    for d in near:
        pl.semaphore_signal(barrier, inc=1, device_id=d, device_id_type=MESH)
    pl.semaphore_wait(barrier, len(near))

    started = []

    def send(src, dst, ssem, rsem, d):
        c = pltpu.make_async_remote_copy(src_ref=src, dst_ref=dst, send_sem=ssem, recv_sem=rsem, device_id=d,
                                         device_id_type=MESH)
        c.start()
        started.append(c)
        return c

    copies = {}

    def spread(kind, node):
        follow = a_next if kind == "a" else b_next
        ssem, rsem = (a_send, a_recv) if kind == "a" else (b_send, b_recv)
        rows = pl.ds(0, HALF) if kind == "a" else pl.ds(HALF, HALF)
        src = kv_ref.at[rows] if node == (0, 0) else kvb.at[node[0] * NZ + node[1], rows]
        for axis, step, dx, dz in follow(*node):
            r = dx * NZ + dz
            copies[(kind, dx, dz)] = send(src, kvb.at[r, rows], ssem.at[r], rsem.at[r], dev(axis, step))

    spread("b", (0, 0))
    spread("a", (0, 0))
    slot = y * 2 + h
    own_rows = pl.ds(pl.multiple_of(slot * ROWS, ROWS), ROWS)
    owns = []
    for i, k in enumerate(range(1, NY)):
        for j, hh in enumerate((h, 1 - h)):
            owns.append(send(kv_ref, kvown.at[own_rows], own_send.at[i * 2 + j], own_recv.at[i * 2 + j],
                             (dev("y", k)[0], hh)))
    owns.append(send(kv_ref, kvown.at[own_rows], own_send.at[6], own_recv.at[6], partner))
    kvown[own_rows] = kv_ref[...]
    kvb[0] = kv_ref[...]

    q = jnp.concatenate([q_ref[:, :DH], q_ref[:, DH:]], axis=0)
    scale = DH ** -0.5

    def scores(keys):
        return lax.dot_general(q, keys, (((1,), (1,)), ((), ())), preferred_element_type=jnp.float32) * scale

    def fold(state, sc, values):
        top = jnp.max(sc, axis=1, keepdims=True)
        if state is not None:
            top = jnp.maximum(top, state[0])
        expo = jnp.exp(sc - top)
        total = jnp.sum(expo, axis=1, keepdims=True)
        acc = jnp.dot(expo.astype(jnp.bfloat16), values, preferred_element_type=jnp.float32)
        if state is not None:
            factor = jnp.exp(state[0] - top)
            total = total + state[1] * factor
            acc = acc + state[2] * factor
        return (top, total, acc)

    cost_a, cost_b = levels(a_next), levels(b_next)
    todo = [(c, 0, "a", n) for n, c in cost_a.items() if c] + [(c, 1, "b", n) for n, c in cost_b.items() if c]
    todo.sort(key=lambda t: (t[0], t[1]))
    state = None
    for cost, _, kind, node in todo:
        if cost == 4 and state is None:
            for c in owns:
                c.wait_recv()
            sc = scores(kvown[:, :DH])
            row = lax.broadcasted_iota(jnp.int32, sc.shape, 0) % (2 * ROWS) + y * (2 * ROWS)
            col = lax.broadcasted_iota(jnp.int32, sc.shape, 1)
            state = fold(None, jnp.where(col <= row, sc, NEG), kvown[:, DH:])
        copies[(kind,) + node].wait_recv()
        spread(kind, node)

    my_rows = pl.ds(pl.multiple_of(h * ROWS, ROWS), ROWS)

    def rel(block):
        block = jnp.maximum(block, 0)
        bx = block // NZ
        bz = block % NZ
        return ((x - bx + NX) % NX) * NZ + (z - bz + NZ) % NZ

    for k in (2, 1, 3, 0):
        span = base + (y + k) % NY
        for j in range(2):
            part = kvb[rel(sel_ref[span, j + 1])]
            if k:
                stg[k - 1, j] = part
            else:
                kvsel[0, j, my_rows] = part
    ys = {}
    for k in (2, 1, 3):
        ys[k] = send(stg.at[k - 1], kvsel.at[k, :, my_rows], y_send.at[k], y_recv.at[k], dev("y", k))
    ps = {0: send(kvsel.at[0, :, my_rows], kvsel.at[0, :, my_rows], p_send.at[0], p_recv.at[0], partner)}

    valid = [sel_ref[s, j + 1] >= 0 for j in range(2)]
    for k in (1, 3, 2):
        ys[k].wait_recv()
        ps[k] = send(kvsel.at[k, :, my_rows], kvsel.at[k, :, my_rows], p_send.at[k], p_recv.at[k], partner)
    for k in (0, 1, 3, 2):
        ps[k].wait_recv()
        kv = kvsel[k].reshape(4 * ROWS, 2 * DH)
        sc = scores(kv[:, :DH])
        col = lax.broadcasted_iota(jnp.int32, sc.shape, 1)
        ok = jnp.where(col < 2 * ROWS, valid[0].astype(jnp.int32), valid[1].astype(jnp.int32))
        state = fold(state, jnp.where(ok > 0, sc, NEG), kv[:, DH:])

    out = state[2] / state[1]
    o_ref[:, :DH] = out[:2 * ROWS].astype(jnp.bfloat16)
    o_ref[:, DH:] = out[2 * ROWS:].astype(jnp.bfloat16)
    for c in started:
        c.wait_send()


def shards(queries, keys_values, selected):
    dma = pltpu.SemaphoreType.DMA
    return pl.pallas_call(
        kernel,
        out_shape=jax.ShapeDtypeStruct(queries.shape, jnp.bfloat16),
        in_specs=[pl.BlockSpec(memory_space=pltpu.VMEM)] * 2 + [pl.BlockSpec(memory_space=pltpu.SMEM)],
        out_specs=pl.BlockSpec(memory_space=pltpu.VMEM),
        scratch_shapes=[
            pltpu.VMEM((NX * NZ, ROWS, 2 * DH), jnp.bfloat16),
            pltpu.VMEM((8 * ROWS, 2 * DH), jnp.bfloat16),
            pltpu.VMEM((NY, 2, 2 * ROWS, 2 * DH), jnp.bfloat16),
            pltpu.VMEM((NY - 1, 2, ROWS, 2 * DH), jnp.bfloat16),
            dma((NX * NZ,)), dma((NX * NZ,)), dma((NX * NZ,)), dma((NX * NZ,)),
            dma((7,)), dma((7,)), dma((NY,)), dma((NY,)), dma((NY,)), dma((NY,)),
        ],
        compiler_params=pltpu.CompilerParams(collective_id=0, has_side_effects=True),
    )(queries, keys_values, selected)


def solution(mesh):
    in_specs = (P("seq", "head"), P(("seq", "head"), None), P())
    out_specs = P("seq", "head")
    return jax.shard_map(shards, mesh=mesh, in_specs=in_specs, out_specs=out_specs, check_vma=False)
```

```python
import jax
import jax.numpy as jnp
from jax import lax
from jax.experimental import pallas as pl
from jax.experimental.pallas import tpu as pltpu
from jax.sharding import PartitionSpec as P

DH = 128
NX, NZ, NY = 4, 8, 4
ROWS = 64
PART = ROWS // NX
MESH = pl.DeviceIdType.MESH
NEG = -1e30


def hops(step, size):
    return min(step % size, -step % size)


def kernel(q_hbm, kv_hbm, sel_hbm, o_ref, q_ref, kv_ref, sel_ref, kvb, kvown, kvsel, stg, in_sem, a_send, a_recv,
           own_send, own_recv, b_send, b_recv, p_send, p_recv):
    s = lax.axis_index("seq")
    h = lax.axis_index("head")
    x = s // (NZ * NY)
    z = (s // NY) % NZ
    y = s % NY

    loads = [pltpu.make_async_copy(a, b, in_sem.at[i])
             for i, (a, b) in enumerate(((kv_hbm, kv_ref), (sel_hbm, sel_ref), (q_hbm, q_ref)))]
    for c in loads:
        c.start()

    def seq_of(ax, az, ay):
        return (x + ax) % NX * (NZ * NY) + (z + az) % NZ * NY + (y + ay) % NY

    plane = [(ax, az) for ax in range(NX) for az in range(NZ) if (ax, az) != (0, 0)]
    plane.sort(key=lambda t: -(hops(t[0], NX) + hops(t[1], NZ)))
    group = [(ax, ay) for ax in range(NX) for ay in range(NY)]
    group.sort(key=lambda t: hops(t[0], NX) + hops(t[1], NY))
    partner = (s, 1 - h)

    near = [(seq_of(ax, az, 0), h) for ax, az in plane]
    near += [(seq_of(ax, 0, ay), h) for ax, ay in group if ay]
    near += [(seq_of(0, 0, ay), 1 - h) for ay in range(1, NY)] + [partner]
    barrier = pltpu.get_barrier_semaphore()
    for d in near:
        pl.semaphore_signal(barrier, inc=1, device_id=d, device_id_type=MESH)
    loads[0].wait()
    pl.semaphore_wait(barrier, len(near))

    started = []

    def send(src, dst, ssem, rsem, d):
        c = pltpu.make_async_remote_copy(src_ref=src, dst_ref=dst, send_sem=ssem, recv_sem=rsem, device_id=d,
                                         device_id_type=MESH)
        c.start()
        started.append(c)
        return c

    firsts = []
    for ax, az in plane:
        r = ax * NZ + az
        rows = pl.ds(pl.multiple_of((x + ax) % NX * PART, PART), PART)
        firsts.append(send(kv_ref.at[rows], kvb.at[r], a_send.at[r], a_recv.at[r], (seq_of(ax, az, 0), h)))
    slot = y * 2 + h
    own_rows = pl.ds(pl.multiple_of(slot * ROWS, ROWS), ROWS)
    owns = []
    for ay in range(NY):
        for j, hh in enumerate((h, 1 - h)):
            if ay or j:
                i = ay * 2 + j
                owns.append(send(kv_ref, kvown.at[own_rows], own_send.at[i], own_recv.at[i], (seq_of(0, 0, ay), hh)))
    kvown[own_rows] = kv_ref[...]
    kvb[0] = kv_ref[pl.ds(pl.multiple_of(x * PART, PART), PART)]

    loads[1].wait()
    loads[2].wait()

    def rel(block):
        block = jnp.maximum(block, 0)
        return (x - block // NZ + NX) % NX * NZ + (z - block % NZ + NZ) % NZ

    picks = []
    for ax, ay in group:
        span = seq_of(ax, 0, ay)
        picks.append([rel(sel_ref[j + 1, span]) for j in range(2)])
    valid = [sel_ref[j + 1, s] for j in range(2)]

    q = jnp.concatenate([q_ref[:, :DH], q_ref[:, DH:]], axis=0)
    scale = DH ** -0.5

    def scores(keys):
        return lax.dot_general(q, keys, (((1,), (1,)), ((), ())), preferred_element_type=jnp.float32) * scale

    def fold(state, sc, values):
        top = jnp.max(sc, axis=1, keepdims=True)
        if state is not None:
            top = jnp.maximum(top, state[0])
        expo = jnp.exp(sc - top)
        total = jnp.sum(expo, axis=1, keepdims=True)
        acc = jnp.dot(expo.astype(jnp.bfloat16), values, preferred_element_type=jnp.float32)
        if state is not None:
            factor = jnp.exp(state[0] - top)
            total = total + state[1] * factor
            acc = acc + state[2] * factor
        return (top, total, acc)

    for c in owns:
        c.wait_recv()
    sc = scores(kvown[:, :DH])
    row = lax.broadcasted_iota(jnp.int32, sc.shape, 0) % (2 * ROWS) + y * (2 * ROWS)
    col = lax.broadcasted_iota(jnp.int32, sc.shape, 1)
    state = fold(None, jnp.where(col <= row, sc, NEG), kvown[:, DH:])

    for c in firsts[::-1]:
        c.wait_recv()

    count = len(group)
    for i in range(count - 1, -1, -1):
        for j in range(2):
            part = kvb[picks[i][j]]
            if i:
                stg[i, j] = part
            else:
                kvsel[j, 0, h] = part
    seconds = {}
    for i in range(count - 1, 0, -1):
        ax, ay = group[i]
        seconds[i] = send(stg.at[i], kvsel.at[:, i, h], b_send.at[i], b_recv.at[i], (seq_of(ax, 0, ay), h))
    thirds = {}
    for i in range(count):
        if i:
            seconds[i].wait_recv()
        thirds[i] = send(kvsel.at[:, i, h], kvsel.at[:, i, h], p_send.at[i], p_recv.at[i], partner)

    lot = count // 2
    for half in range(2):
        for i in range(half * lot, half * lot + lot):
            thirds[i].wait_recv()
        kv = kvsel[:, half * lot:half * lot + lot].reshape(2 * lot * 2 * PART, 2 * DH)
        sc = scores(kv[:, :DH])
        col = lax.broadcasted_iota(jnp.int32, sc.shape, 1)
        ok = jnp.where(col < lot * 2 * PART, valid[0], valid[1])
        state = fold(state, jnp.where(ok >= 0, sc, NEG), kv[:, DH:])

    out = state[2] / state[1]
    o_ref[:, :DH] = out[:2 * ROWS].astype(jnp.bfloat16)
    o_ref[:, DH:] = out[2 * ROWS:].astype(jnp.bfloat16)
    for c in started:
        c.wait_send()


def shards(queries, keys_values, selected):
    dma = pltpu.SemaphoreType.DMA
    count = NX * NY
    return pl.pallas_call(
        kernel,
        out_shape=jax.ShapeDtypeStruct(queries.shape, jnp.bfloat16),
        in_specs=[pl.BlockSpec(memory_space=pl.ANY)] * 3,
        out_specs=pl.BlockSpec(memory_space=pltpu.VMEM),
        scratch_shapes=[
            pltpu.VMEM(queries.shape, jnp.bfloat16),
            pltpu.VMEM(keys_values.shape, jnp.bfloat16),
            pltpu.SMEM((3, NX * NZ * NY), jnp.int32),
            pltpu.VMEM((NX * NZ, PART, 2 * DH), jnp.bfloat16),
            pltpu.VMEM((8 * ROWS, 2 * DH), jnp.bfloat16),
            pltpu.VMEM((2, count, 2, PART, 2 * DH), jnp.bfloat16),
            pltpu.VMEM((count, 2, PART, 2 * DH), jnp.bfloat16),
            dma((3,)), dma((NX * NZ,)), dma((NX * NZ,)), dma((8,)), dma((8,)), dma((count,)), dma((count,)),
            dma((count,)), dma((count,)),
        ],
        compiler_params=pltpu.CompilerParams(collective_id=0, has_side_effects=True),
    )(queries, keys_values, selected.T)


def solution(mesh):
    in_specs = (P("seq", "head"), P(("seq", "head"), None), P())
    out_specs = P("seq", "head")
    return jax.shard_map(shards, mesh=mesh, in_specs=in_specs, out_specs=out_specs, check_vma=False)
```
